32 devices in a mesh: dp: 8 (over y, x, core), rep: 4 (over z).
Axes of the slice: x: 2, y: 2, z: 4, core: 2. Of those that a mesh axis runs over, the one named last changes fastest.
Arguments:
- images: bfloat16 [64, 8, 8, 3072], P(('dp', 'rep')), may hold values from -15 to 15
- depth_kernel: float32 [49, 3072], replicated, may hold values from -0.875 to 0.875
- norm_gain: float32 [3072], replicated, may hold values from 0.1 to 1.9
- expand_weight: bfloat16 [3072, 6144], P('dp', 'rep'), may hold values from -0.109375 to 0.109375
- contract_weight: bfloat16 [6144, 3072], P('rep', 'dp'), may hold values from -0.078125 to 0.078125
- layer_scale: float32 [3072], replicated, may hold values from 0.3 to 1.5
- head_gain: float32 [3072], replicated, may hold values from 0.5 to 1.5
- head_weight: bfloat16 [3072, 1024], P('dp', 'rep'), may hold values from -0.108253175 to 0.108253175
- caption_embed: bfloat16 [64, 1024], P(('dp', 'rep')), may hold values from -32 to 32
- logit_scale: float32 [1], replicated, may hold values from 4.5 to 4.605
- pair_labels: int32 [64], P(('dp', 'rep')), may hold values from 0 to 63, as said below
Outputs:
- image_proj: float32 [64, 1024], P(('dp', 'rep'))
- pair_loss: float32 [64], P(('dp', 'rep'))
The draws below stay inside these ranges and needn't reach their ends.
Inputs may be any that keep to these rules, and one draw needn't show every extreme that they name: pair_labels names every caption row exactly once.
All inputs are finite; a program needn't handle non-finite values.
Results may differ from the reference program's by a relative error of at most 0.004.
Values may be sent and summed in bfloat16 or wider, within the bound.
No kernel may reach another device: no remote copies, remote signals or barrier semaphores. Data moves between devices by JAX's collectives and lax.ppermute only.
A program may use at most 128 MiB of HBM per device.

```python
import math
import jax
import jax.numpy as jnp
from jax import lax

C = 3072
FF = 6144
E = 1024
SIDE = 8
IMG_DEV = 2
IMAGES = 64
N_REP = 4


def content_rows(key):
    values = jax.random.normal(jax.random.fold_in(key, 11), (IMAGES, C), jnp.float32)
    return jnp.clip(3.0 * values, -10.0, 10.0)


def head_matrix(key):
    values = jax.random.normal(jax.random.fold_in(key, 12), (C, E), jnp.float32)
    return jnp.clip(values, -6.0, 6.0) * C ** (-0.5)


def caption_order(key):
    return jax.random.permutation(jax.random.fold_in(key, 13), IMAGES).astype(jnp.int32)


def draw_images(key, part):
    content = content_rows(key)
    noise = jnp.clip(jax.random.normal(jax.random.fold_in(key, 14), (IMAGES, SIDE, SIDE, C), jnp.float32), -5.0, 5.0)
    return (content[:, None, None, :] + noise).astype(jnp.bfloat16)


def draw_head_weight(key, part):
    return head_matrix(key).astype(jnp.bfloat16)


def draw_pair_labels(key, part):
    return caption_order(key)


def draw_logit_scale(key, part):
    return jax.random.uniform(jax.random.fold_in(key, 21), (1,), jnp.float32, 4.5, 4.605)


def draw_caption_embed(key, part):
    aligned = jnp.dot(content_rows(key), head_matrix(key), precision=lax.Precision.HIGHEST) / 3.0
    aligned = jnp.clip(aligned, -6.0, 6.0)
    pick = jax.random.uniform(jax.random.fold_in(key, 16), (IMAGES,), jnp.float32)
    level = jax.random.uniform(jax.random.fold_in(key, 17), (IMAGES,), jnp.float32)
    strength = jnp.where(pick < 0.25, 0.3 * level, 0.6 + 0.39 * level)
    noise = jnp.clip(jax.random.normal(jax.random.fold_in(key, 20), (IMAGES, E), jnp.float32), -5.0, 5.0)
    row_scale = jnp.exp(jax.random.uniform(jax.random.fold_in(key, 22), (IMAGES,), jnp.float32, -0.2, 0.2))
    twin = jax.random.uniform(jax.random.fold_in(key, 18), (IMAGES,), jnp.float32) < 0.12
    spacing = 0.01 + 0.02 * jax.random.uniform(jax.random.fold_in(key, 19), (IMAGES,), jnp.float32)
    follow = jnp.roll(twin & (strength > 0.5), 1)
    share = jnp.where(follow, jnp.roll(strength - spacing, 1), strength)
    aim = jnp.where(follow[:, None], jnp.roll(aligned, 1, axis=0), aligned)
    rows = (share[:, None] * aim + jnp.sqrt(1.0 - share * share)[:, None] * noise) * row_scale[:, None]
    placed = jnp.zeros((IMAGES, E), jnp.float32).at[caption_order(key)].set(rows)
    return placed.astype(jnp.bfloat16)


def shard_levels(rng, dims, pieces, least, high):
    def one(position, shards_of):
        draws = jax.random.uniform(jax.random.fold_in(jax.random.fold_in(rng, 6), position), (shards_of,), jnp.float32, least / len(pieces), high / len(pieces))
        return jnp.repeat(jnp.exp(draws), dims[position] // shards_of).reshape((-1,) + (1,) * (len(dims) - position - 1))

    level = one(*pieces[0])
    for cut in pieces[1:]:
        level = level * one(*cut)
    return level


def normal_values(rng, dims, scale, reach, cuts=(), dtype=jnp.bfloat16):
    result = scale * jax.random.normal(rng, dims, jnp.float32)
    if cuts:
        result = result * shard_levels(rng, dims, cuts, -0.22, 0.18)
    return jnp.clip(result, -reach, reach).astype(dtype)


def setup_inputs(seed: int = 0) -> dict:
    key_of = jax.random.split(jax.random.key(seed), 12)
    return {
        "images": draw_images(jax.random.fold_in(key_of[11], 71), 0),
        "depth_kernel": normal_values(key_of[1], (49, C), 49 ** -0.5, 0.875, (), jnp.float32),
        "norm_gain": jnp.clip(1.0 + 0.18 * jax.random.normal(key_of[2], (C,), jnp.float32), 0.1, 1.9),
        "expand_weight": normal_values(key_of[3], (C, FF), C ** -0.5, 0.109375, ((0, 8), (1, 4))),
        "contract_weight": normal_values(key_of[4], (FF, C), FF ** -0.5, 0.078125, ((0, 4), (1, 8))),
        "layer_scale": jnp.clip(jnp.exp(jax.random.uniform(key_of[5], (C,), jnp.float32, math.log(0.3), math.log(1.5))), 0.3, 1.5),
        "head_gain": jnp.clip(1.0 + 0.1 * jax.random.normal(key_of[6], (C,), jnp.float32), 0.5, 1.5),
        "head_weight": draw_head_weight(jax.random.fold_in(key_of[11], 71), 0),
        "caption_embed": draw_caption_embed(jax.random.fold_in(key_of[11], 71), 0),
        "logit_scale": draw_logit_scale(jax.random.fold_in(key_of[11], 71), 0),
        "pair_labels": draw_pair_labels(jax.random.fold_in(key_of[11], 71), 0),
    }


def layer_norm(values, gain):
    centre = values - lax.optimization_barrier(jnp.mean(values, axis=-1, keepdims=True))
    spread = lax.optimization_barrier(jnp.mean(centre * centre, axis=-1, keepdims=True))
    return centre * lax.rsqrt(spread + 1e-06) * gain

def block_pool(group, depth_kernel, norm_gain, expand_weight, contract_weight, layer_scale):
    count = group.shape[0]
    chans = group.shape[3]
    features = group.astype(jnp.float32)
    padded = jnp.pad(features, ((0, 0), (3, 3), (3, 3), (0, 0)))
    conv = jnp.zeros_like(features)
    for tap_a in range(7):
        for tap_b in range(7):
            conv = conv + padded[:, tap_a:tap_a + SIDE, tap_b:tap_b + SIDE, :] * depth_kernel[7 * tap_a + tap_b]
    normed = layer_norm(conv, norm_gain).astype(jnp.bfloat16).reshape(count * SIDE * SIDE, chans)
    pre = jnp.dot(normed, expand_weight, preferred_element_type=jnp.float32)
    hidden = jax.nn.gelu(pre, approximate=False).astype(jnp.bfloat16)
    branch = jnp.dot(hidden, contract_weight, preferred_element_type=jnp.float32).reshape(count, SIDE * SIDE, chans)
    return lax.optimization_barrier(jnp.mean(features.reshape(count, SIDE * SIDE, chans) + layer_scale * branch, axis=1))

def reference(images, depth_kernel, norm_gain, expand_weight, contract_weight, layer_scale, head_gain, head_weight, caption_embed, logit_scale, pair_labels):
    group_size = IMG_DEV * N_REP
    blocks = images.reshape(IMAGES // group_size, group_size, SIDE, SIDE, C)
    pooled = lax.map(lambda group: block_pool(group, depth_kernel, norm_gain, expand_weight, contract_weight, layer_scale), blocks)
    pooled = pooled.reshape(IMAGES, C)
    head_in = layer_norm(pooled, head_gain).astype(jnp.bfloat16)
    image_proj = jnp.dot(head_in, head_weight, preferred_element_type=jnp.float32)
    image_unit = (image_proj * lax.rsqrt(lax.optimization_barrier(jnp.sum(image_proj * image_proj, axis=1, keepdims=True)) + 1e-06)).astype(jnp.bfloat16)
    texts = caption_embed.astype(jnp.float32)
    caption_unit = (texts * lax.rsqrt(lax.optimization_barrier(jnp.sum(texts * texts, axis=1, keepdims=True)) + 1e-06)).astype(jnp.bfloat16)
    scores = lax.dot_general(image_unit, caption_unit, (((1,), (1,)), ((), ())), preferred_element_type=jnp.float32)
    logits = jnp.exp(logit_scale[0]) * scores
    target = jnp.take_along_axis(logits, pair_labels[:, None].astype(jnp.int32), axis=1)[:, 0]
    pair_loss = jax.nn.logsumexp(logits, axis=1) - target
    return (image_proj, pair_loss)
```

```python
import functools
import jax
import jax.numpy as jnp
from jax import lax
from jax.experimental import pallas as pl
from jax.experimental.pallas import tpu as pltpu
from jax.sharding import PartitionSpec as P


LANES = 128
F32 = jnp.float32
BF16 = jnp.bfloat16


def split_high_low(x):
    high = x.astype(BF16)
    return high, (x - high.astype(F32)).astype(BF16)


def dot_high_low(x, w):
    high, low = split_high_low(x)
    return jnp.dot(high, w, preferred_element_type=F32) + jnp.dot(
        low, w, preferred_element_type=F32
    )


def conv_norm_kernel(side, x_ref, k_ref, g_ref, out_ref, mean_ref, conv_ref):
    places, chans = out_ref.shape
    chunks = chans // LANES
    reach = 3
    taps = 2 * reach + 1
    col = lax.broadcasted_iota(jnp.int32, (side, LANES), 0)

    def chunk(i, sums):
        lanes = pl.ds(pl.multiple_of(i * LANES, LANES), LANES)
        flat = x_ref[0, :, lanes].astype(F32)
        rows = [flat[side * h : side * (h + 1)] for h in range(side)]
        total = rows[0]
        for h in range(1, side):
            total = total + rows[h]
        mean_ref[0, :, lanes] = jnp.sum(total, axis=0, keepdims=True) * (1.0 / places)
        conv = [jnp.zeros((side, LANES), F32) for _ in range(side)]
        for b in range(taps):
            d = b - reach
            if d == 0:
                moved = rows
            else:
                keep = (col + d >= 0) & (col + d < side)
                moved = [
                    jnp.where(keep, pltpu.roll(r, (-d) % side, 0), 0.0) for r in rows
                ]
            for a in range(taps):
                tap = jnp.broadcast_to(k_ref[pl.ds(taps * a + b, 1), lanes], (side, LANES))
                for h in range(side):
                    src = h + a - reach
                    if 0 <= src < side:
                        conv[h] = conv[h] + moved[src] * tap
        for h in range(side):
            conv_ref[side * h : side * (h + 1), lanes] = conv[h]
        return tuple(s + c for s, c in zip(sums, conv))

    zeros = tuple(jnp.zeros((side, LANES), F32) for _ in range(side))
    sums = lax.fori_loop(0, chunks, chunk, zeros)
    mean = [jnp.sum(s, axis=1, keepdims=True) * (1.0 / chans) for s in sums]

    def second(i, sums):
        lanes = pl.ds(pl.multiple_of(i * LANES, LANES), LANES)
        out = []
        for h in range(side):
            c = conv_ref[side * h : side * (h + 1), lanes] - mean[h]
            out.append(sums[h] + c * c)
        return tuple(out)

    sums = lax.fori_loop(0, chunks, second, zeros)
    scale = [
        lax.rsqrt(jnp.sum(s, axis=1, keepdims=True) * (1.0 / chans) + 1e-06) for s in sums
    ]

    def third(i, carry):
        lanes = pl.ds(pl.multiple_of(i * LANES, LANES), LANES)
        gain = g_ref[:, lanes]
        for h in range(0, side, 2):
            pair = [
                (conv_ref[side * q : side * (q + 1), lanes] - mean[q]) * scale[q] * gain
                for q in (h, h + 1)
            ]
            out_ref[side * h : side * (h + 2), lanes] = jnp.concatenate(pair, axis=0).astype(BF16)
        return carry

    lax.fori_loop(0, chunks, third, 0)


def conv_norm(images, depth_kernel, norm_gain, n):
    count, side, _, chans = images.shape
    places = side * side
    flat = images.reshape(count, places, chans)
    return pl.pallas_call(
        functools.partial(conv_norm_kernel, side),
        grid=(1,),
        in_specs=[
            pl.BlockSpec((1, places, chans), lambda s: (n, 0, 0)),
            pl.BlockSpec(depth_kernel.shape, lambda s: (0, 0)),
            pl.BlockSpec((1, chans), lambda s: (0, 0)),
        ],
        out_specs=[
            pl.BlockSpec((places, chans), lambda s: (0, 0)),
            pl.BlockSpec((1, 1, chans), lambda s: (0, 0, 0)),
        ],
        out_shape=[
            jax.ShapeDtypeStruct((places, chans), BF16),
            jax.ShapeDtypeStruct((1, 1, chans), F32),
        ],
        scratch_shapes=[pltpu.VMEM((places, chans), F32)],
        name=f"conv_norm_{n}",
    )(flat, depth_kernel, norm_gain.reshape(1, chans))


def erf(x):
    return lax.erf(x)


def expand_kernel(places, chunks, pieces, info_ref, *refs):
    n_chunk_refs = sum(len(c) for c in chunks)
    chunk_refs = refs[:n_chunk_refs]
    piece_refs = refs[n_chunk_refs : n_chunk_refs + len(pieces)]
    out_ref = refs[n_chunk_refs + len(pieces)]
    rows_ref, sems = refs[n_chunk_refs + len(pieces) + 1 :]
    step = pl.program_id(0)

    @pl.when(step == 0)
    def _():
        at = 0
        copies = []
        for c, alternatives in enumerate(chunks):
            dst = rows_ref.at[pl.ds(c * places, places), :]
            for q in range(len(alternatives)):
                copy = pltpu.make_async_copy(chunk_refs[at + q], dst, sems.at[c])
                if len(alternatives) == 1:
                    copy.start()
                else:
                    pl.when(info_ref[1] == q)(copy.start)
            copies.append(pltpu.make_async_copy(chunk_refs[at], dst, sems.at[c]))
            at += len(alternatives)
        for copy in copies:
            copy.wait()

    total = None
    for (mask, half), ref in zip(pieces, piece_refs):
        depth = ref.shape[0]
        if half == 2:
            continue
        weight = ref[...]
        if half == 1:
            other = piece_refs[pieces.index((mask, 2))]
            weight = jnp.where(step < pl.num_programs(0) // 2, weight, other[...])
        start = pl.multiple_of((info_ref[0] ^ mask) * depth, LANES)
        part = jnp.dot(rows_ref[:, pl.ds(start, depth)], weight, preferred_element_type=F32)
        total = part if total is None else total + part
    hidden = 0.5 * total * (1.0 + erf(total * (0.5**0.5)))
    hidden = hidden.astype(BF16).astype(F32)
    for c in range(len(chunks)):
        out_ref[pl.ds(c, 1), :] = jnp.sum(
            hidden[c * places : (c + 1) * places], axis=0, keepdims=True
        ) * (1.0 / places)


def expand(info, chunks, pieces, width, name):
    places, chans = chunks[0][0].shape
    block = 256
    steps = width // block
    keys = tuple(k for k, _ in pieces)

    def spec(key, w):
        half = key[1]
        if half == 0:
            index = lambda s, info: (0, s)
        elif half == 1:
            index = lambda s, info: (0, jnp.minimum(s, steps // 2 - 1))
        else:
            index = lambda s, info: (0, jnp.maximum(s - steps // 2, 0))
        return pl.BlockSpec((w.shape[0], block), index)

    flat = [a for c in chunks for a in c]
    return pl.pallas_call(
        functools.partial(expand_kernel, places, tuple((0,) * len(c) for c in chunks), keys),
        grid_spec=pltpu.PrefetchScalarGridSpec(
            num_scalar_prefetch=1,
            grid=(steps,),
            in_specs=[pl.BlockSpec(memory_space=pl.ANY) for _ in flat]
            + [spec(k, w) for k, w in pieces],
            out_specs=pl.BlockSpec((len(chunks), block), lambda s, info: (0, s)),
            scratch_shapes=[
                pltpu.VMEM((len(chunks) * places, chans), BF16),
                pltpu.SemaphoreType.DMA((len(chunks),)),
            ],
        ),
        out_shape=jax.ShapeDtypeStruct((len(chunks), width), F32),
        compiler_params=pltpu.CompilerParams(vmem_limit_bytes=40 << 20),
        name=name,
    )(info, *flat, *[w for _, w in pieces])


def body(
    n_dp,
    n_rep,
    images,
    depth_kernel,
    norm_gain,
    expand_weight,
    contract_weight,
    layer_scale,
    head_gain,
    head_weight,
    caption_embed,
    logit_scale,
    pair_labels,
):
    count, side, _, chans = images.shape
    places = side * side
    width = expand_weight.shape[1]
    block = chans // n_dp
    cols = head_weight.shape[1]
    every = n_dp * n_rep
    me_dp = lax.axis_index("dp")
    me_rep = lax.axis_index("rep")
    cube = n_dp == 2**3
    line = n_rep == 2**2

    def swap(x, axis, mask):
        size = n_dp if axis == "dp" else n_rep
        return lax.ppermute(x, axis, [(q, q ^ mask) for q in range(size)])

    def middle(x):
        return lax.ppermute(x, "rep", [(0, 0), (1, 2), (2, 1), (3, 3)])

    own, means = [], []
    for n in range(count):
        normed, mean = conv_norm(images, depth_kernel, norm_gain, n)
        own.append(normed)
        means.append(mean.reshape(1, chans))
    if cube:
        half = width // 2
        wx = swap(expand_weight, "dp", 2)
        wy = swap(expand_weight, "dp", 4)
        dx = swap(wy[:, :half], "dp", 2)
        dy = swap(wx[:, half:], "dp", 4)
        pieces = [((0, 0), expand_weight), ((2, 0), wx), ((4, 0), wy), ((6, 1), dx), ((6, 2), dy)]
        pieces += [((k[0] ^ 1, k[1]), swap(w, "dp", 1)) for k, w in pieces]
        base = me_dp
    else:
        pieces = [((0, 0), lax.all_gather(expand_weight, "dp", axis=0, tiled=True))]
        base = jnp.zeros_like(me_dp)
    is_middle = ((me_rep == 1) | (me_rep == 2)).astype(jnp.int32)
    info = jnp.stack([base.astype(jnp.int32), is_middle])
    if line:
        first = [swap(x, "rep", 1) for x in own]
        b = [middle(x) for x in own]
        c = [swap(x, "rep", 1) for x in b]
        d = [middle(x) for x in first]
        e = [swap(x, "rep", 1) for x in d]
        early = [[x] for x in own] + [[x] for x in first] + [[p, q] for p, q in zip(c, b)]
        late = [[p, q] for p, q in zip(e, d)]
        hm_early = expand(info, early, pieces, width, "expand_early")
        hm_late = expand(info, late, pieces, width, "expand_late")
        third = hm_early[2 * count :]
        slots = [hm_early[:count], hm_early[count : 2 * count]]
        flag = is_middle > 0
        slots += [jnp.where(flag, hm_late, third), jnp.where(flag, third, hm_late)]
        by_xor = jnp.stack(slots)
        hidden_mean = jnp.stack(
            [lax.dynamic_index_in_dim(by_xor, me_rep ^ r, 0, keepdims=False) for r in range(n_rep)]
        )
    else:
        rows = lax.all_gather(jnp.stack(own), "rep", axis=0, tiled=True)
        hm = expand(info, [[rows[q]] for q in range(n_rep * count)], pieces, width, "expand_all")
        hidden_mean = hm.reshape(n_rep, count, width)
    hidden_mean = hidden_mean.reshape(n_rep * count, width)

    image_mean = jnp.concatenate(means, axis=0)
    sent = image_mean.reshape(count, n_dp, block).transpose(1, 0, 2)
    rep_mean = lax.all_to_all(sent, "dp", 0, 0, tiled=True)
    slices = [swap(rep_mean, "rep", q) if q else rep_mean for q in range(n_rep)]
    by_xor = jnp.stack(slices)
    all_mean = jnp.stack(
        [lax.dynamic_index_in_dim(by_xor, me_rep ^ r, 0, keepdims=False) for r in range(n_rep)],
        axis=1,
    ).reshape(every * count, block)

    texts = caption_embed.astype(F32)
    caption_unit = (
        texts * lax.rsqrt(jnp.sum(texts * texts, axis=1, keepdims=True) + 1e-06)
    ).astype(BF16)
    every_caption = lax.all_gather(caption_unit, ("dp", "rep"), axis=0, tiled=True)

    all_hidden = lax.all_gather(hidden_mean, "dp", axis=0, tiled=True)
    slab = dot_high_low(all_hidden, contract_weight)
    total = slab
    for q in range(1, n_rep):
        total = total + swap(slab, "rep", q)
    mine = pl.ds(me_dp * block, block)
    scale = lax.dynamic_slice_in_dim(layer_scale, me_dp * block, block)
    gain = lax.dynamic_slice_in_dim(head_gain, me_dp * block, block)
    pooled = all_mean + scale * total

    part_mean = jnp.mean(pooled, axis=1, keepdims=True)
    centred = pooled - part_mean
    part_var = jnp.sum(centred * centred, axis=1, keepdims=True)
    part_proj = dot_high_low(centred * gain, head_weight)
    gain_proj = jnp.sum(gain[:, None] * head_weight.astype(F32), axis=0)
    stats = jnp.concatenate([part_mean, part_var], axis=1).reshape(every, 1, 2 * count)
    stats = jnp.pad(stats, ((0, 0), (0, 0), (0, cols - 2 * count)))
    message = jnp.concatenate(
        [
            part_proj.reshape(every, count, cols),
            jnp.broadcast_to(gain_proj, (every, 1, cols)),
            stats,
        ],
        axis=1,
    )
    got = lax.all_to_all(message, ("dp", "rep"), 0, 0, tiled=True)
    got = got.reshape(n_dp, n_rep, count + 2, cols)
    numbers = got[:, 0, count + 1, : 2 * count].reshape(n_dp, count, 2)
    means_i, vars_i = numbers[..., 0], numbers[..., 1]
    mean = jnp.mean(means_i, axis=0)
    off = means_i - mean
    var = jnp.sum(vars_i + block * off * off, axis=0) * (1.0 / chans)
    proj = jnp.sum(
        got[:, :, :count] + off[:, None, :, None] * got[:, :, count : count + 1], axis=0
    )
    image_proj = proj.transpose(1, 0, 2).reshape(count, n_rep * cols)
    image_proj = image_proj * lax.rsqrt(var + 1e-06)[:, None]

    image_unit = (
        image_proj * lax.rsqrt(jnp.sum(image_proj * image_proj, axis=1, keepdims=True) + 1e-06)
    ).astype(BF16)
    temper = jnp.exp(logit_scale[0])
    logits = temper * lax.dot_general(
        image_unit, every_caption, (((1,), (1,)), ((), ())), preferred_element_type=F32
    )
    column_ids = lax.broadcasted_iota(jnp.int32, logits.shape, 1)
    target = jnp.sum(jnp.where(column_ids == pair_labels[:, None], logits, 0.0), axis=1)
    pair_loss = jax.nn.logsumexp(logits, axis=1) - target
    return (image_proj, pair_loss)


def solution(mesh):
    return jax.shard_map(
        functools.partial(body, mesh.shape["dp"], mesh.shape["rep"]),
        mesh=mesh,
        in_specs=(
            P(("dp", "rep"), None, None, None),
            P(),
            P(),
            P("dp", "rep"),
            P("rep", "dp"),
            P(),
            P(),
            P("dp", "rep"),
            P(("dp", "rep"), None),
            P(),
            P(("dp", "rep")),
        ),
        out_specs=(P(("dp", "rep"), None), P(("dp", "rep"))),
        check_vma=False,
    )
```
